32 devices in a mesh: seq: 8 (over z, y), grp: 4 (over x, core).
Axes of the slice: x: 2, y: 2, z: 4, core: 2. Of those that a mesh axis runs over, the one named last changes fastest.
Arguments:
- queries: bfloat16 [2048, 5120], P('seq', 'grp'), may hold values from -64 to 64
- keys: bfloat16 [2048, 5120], P('seq', 'grp'), may hold values from -4 to 4
- values: bfloat16 [2048, 5120], P('seq', 'grp'), may hold values from -24 to 24
- cluster_of: int32 [2048], P('seq'), may hold values from 0 to 15, as said below
- pair_mask: int32 [16, 16], replicated, may hold values from 0 to 1, as said below
- out_weight: bfloat16 [5120, 5120], P('grp'), may hold values from -0.078125 to 0.078125
Outputs:
- mixed: bfloat16 [2048, 5120], P('seq', 'grp')
The draws below stay inside these ranges and needn't reach their ends.
Inputs may be any that keep to these rules, and one draw needn't show every extreme that they name: `cluster_of`: of the 256 tokens at one index of seq, at most 64 have a cluster c with c // 2 equal to any one j, and in every draw some index sends exactly 64 to some j. A cluster holds at most 256 tokens, and in every draw some cluster holds exactly 256. pair_mask[c, c] = 1 for every cluster c.
All inputs are finite; a program needn't handle non-finite values.
Results may differ from the reference program's by a relative error of at most 0.013.
Values may be sent and summed in bfloat16 or wider, within the bound.
A program may use at most 128 MiB of HBM per device.

```python
import jax
import jax.numpy as jnp
from jax import lax

D = 5120
H = 40
HD = 128
TOK_DEV = 256
CL_DEV = 2
TOKENS = 2048
NCLUS = 16
CAP = 256
N_SEQ = 8


def cluster_layout(key):
    base_key = jax.random.fold_in(key, 101)
    streams = jax.random.split(base_key, 6)
    mean_count = TOK_DEV // N_SEQ
    shards = N_SEQ
    chosen = jax.random.randint(streams[0], (), 0, shards)
    orders = jax.vmap(lambda subkey: jax.random.permutation(subkey, shards))(jax.random.split(streams[1], shards)).astype(jnp.int32)
    first_owner = orders[:, :1]
    orders = jnp.where(orders == chosen, first_owner, orders)
    orders = orders.at[:, 0].set(chosen)
    shifted = jax.random.randint(streams[2], (shards, shards // 2), 0, mean_count + 1)
    shifted = shifted.at[:, 0].set(mean_count)
    by_place = jnp.stack([mean_count + shifted, mean_count - shifted], axis=2).reshape(shards, shards)
    counts = jnp.zeros((shards, shards), jnp.int32).at[jnp.arange(shards)[:, None], orders].set(by_place)
    cum_ends = jnp.cumsum(counts, axis=1)
    positions = jnp.arange(TOK_DEV, dtype=jnp.int32)
    owner_at = jnp.sum((cum_ends[:, None, :] <= positions[None, :, None]).astype(jnp.int32), axis=2)
    shuffles = jax.vmap(lambda subkey: jax.random.permutation(subkey, TOK_DEV))(jax.random.split(streams[3], shards))
    owner_tok = jnp.take_along_axis(owner_at, shuffles, axis=1).reshape(TOKENS).astype(jnp.int32)
    totals = jnp.sum(counts, axis=0)
    remain = totals
    boundary = jnp.zeros_like(totals)
    bound_list = []
    cut_keys = jax.random.split(streams[4], CL_DEV)
    for part_index in range(CL_DEV - 1):
        lower = jnp.maximum(0, remain - (CL_DEV - 1 - part_index) * CAP)
        upper = jnp.minimum(CAP, remain)
        piece_size = jax.random.randint(cut_keys[part_index], (shards,), lower, upper + 1)
        boundary = boundary + piece_size
        bound_list.append(boundary)
        remain = remain - piece_size
    order_score = jax.random.permutation(streams[5], TOKENS).astype(jnp.int32)
    ordering = jnp.argsort(owner_tok * TOKENS + order_score, stable=True)
    starts = jnp.cumsum(totals) - totals
    sorted_owner = owner_tok[ordering]
    rank_in = jnp.zeros((TOKENS,), jnp.int32).at[ordering].set(jnp.arange(TOKENS, dtype=jnp.int32) - starts[sorted_owner])
    sub_index = jnp.zeros((TOKENS,), jnp.int32)
    for edge_now in bound_list:
        sub_index = sub_index + (rank_in >= edge_now[owner_tok]).astype(jnp.int32)
    return (owner_tok * CL_DEV + sub_index).astype(jnp.int32)


def key_values(key):
    stream = jax.random.fold_in(key, 303)
    base_values = jnp.clip(jax.random.normal(stream, (TOKENS, H * HD), jnp.float32), -4.0, 4.0)
    return base_values


def draw_keys(key, part):
    return key_values(key).astype(jnp.bfloat16)


def draw_queries(key, part):
    stream = jax.random.fold_in(key, 404)
    query_values = 1.5 * jnp.clip(jax.random.normal(stream, (TOKENS, H * HD), jnp.float32), -4.0, 4.0)
    return query_values.astype(jnp.bfloat16)


def draw_cluster_of(key, part):
    return cluster_layout(key)


def draw_pair_mask(key, part):
    stream = jax.random.fold_in(key, 202)
    picked = jax.random.randint(stream, (NCLUS, NCLUS), 0, 4)
    diagonal = jnp.arange(NCLUS)[:, None] == jnp.arange(NCLUS)[None, :]
    return jnp.where((picked == 0) | diagonal, 1, 0).astype(jnp.int32)


def block_levels(stream_key, dims, cuts, smallest, top_value):
    def one(axis_at, parts):
        heights = jax.random.uniform(jax.random.fold_in(jax.random.fold_in(stream_key, 6), axis_at), (parts,), jnp.float32, smallest / len(cuts), top_value / len(cuts))
        return jnp.repeat(jnp.exp(heights), dims[axis_at] // parts).reshape((-1,) + (1,) * (len(dims) - axis_at - 1))

    level = one(*cuts[0])
    for cut in cuts[1:]:
        level = level * one(*cut)
    return level


def scatter_about(own_key, shape, deviation, reach, cuts=(), held_as=jnp.bfloat16):
    drawn = deviation * jax.random.normal(own_key, shape, jnp.float32)
    if cuts:
        drawn = drawn * block_levels(own_key, shape, cuts, -0.22, 0.18)
    return jnp.clip(drawn, -reach, reach).astype(held_as)


def setup_inputs(seed: int = 0) -> dict:
    key_of = jax.random.split(jax.random.key(seed), 7)
    return {
        "queries": draw_queries(jax.random.fold_in(key_of[6], 71), 0),
        "keys": draw_keys(jax.random.fold_in(key_of[6], 71), 0),
        "values": scatter_about(key_of[2], (TOKENS, H * HD), 6.0, 24.0, ((0, 8), (1, 4))),
        "cluster_of": draw_cluster_of(jax.random.fold_in(key_of[6], 71), 0),
        "pair_mask": draw_pair_mask(jax.random.fold_in(key_of[6], 71), 0),
        "out_weight": scatter_about(key_of[5], (H * HD, D), (H * HD) ** -0.5, 0.078125, ((0, 4),)),
    }


def reference(queries, keys, values, cluster_of, pair_mask, out_weight):
    cluster_hot = (cluster_of[:, None] == jnp.arange(NCLUS, dtype=jnp.int32)[None, :]).astype(jnp.float32)
    mask_rows = jnp.dot(cluster_hot, pair_mask.astype(jnp.float32))
    allowed = jnp.dot(mask_rows, cluster_hot.T) > 0.5
    query_heads = queries.reshape(TOKENS, H, HD).transpose(1, 0, 2)
    key_heads = keys.reshape(TOKENS, H, HD).transpose(1, 0, 2)
    value_heads = values.reshape(TOKENS, H, HD).transpose(1, 0, 2)

    def one_head(operands):
        query_part, key_part, value_part = operands
        scores = jnp.dot(query_part, key_part.T, preferred_element_type=jnp.float32) * (HD ** -0.5)
        top_score = jnp.max(jnp.where(allowed, scores, -jnp.inf), axis=1, keepdims=True)
        weights = jnp.where(allowed, jnp.exp(scores - top_score), 0.0)
        row_total = jnp.sum(weights, axis=1, keepdims=True)
        result = jnp.dot(weights.astype(jnp.bfloat16), value_part, preferred_element_type=jnp.float32) / row_total
        return result.astype(jnp.bfloat16)

    per_head = lax.map(one_head, (query_heads, key_heads, value_heads))
    attention = per_head.transpose(1, 0, 2).reshape(TOKENS, H * HD)
    return jnp.dot(attention, out_weight, preferred_element_type=jnp.float32).astype(jnp.bfloat16)
```

```python
import functools

import jax
import jax.numpy as jnp
from jax import lax
from jax.experimental import pallas as pl
from jax.experimental.pallas import tpu as pltpu
from jax.sharding import PartitionSpec as P

HD = 128
NEG = -1e30
LOG2E = 1.4426950408889634
SCALE = HD**-0.5 * LOG2E


def attention_kernel(query, query_bias, key, key_hot, value, out):
    left = jnp.concatenate([query[...], query_bias[...]], axis=1)
    right = jnp.concatenate([key[...], key_hot[...]], axis=1)
    scores = lax.dot_general(
        left, right, (((1,), (1,)), ((), ())), preferred_element_type=jnp.float32
    )
    top = jnp.max(scores, axis=1, keepdims=True) * SCALE
    weights = jnp.exp2(scores * SCALE - top)
    total = jnp.sum(weights, axis=1, keepdims=True)
    mixed = jnp.dot(weights.astype(jnp.bfloat16), value[...], preferred_element_type=jnp.float32)
    out[...] = (mixed / total).astype(jnp.bfloat16)


def attention(queries, query_bias, gathered):
    rows, width = queries.shape
    heads = width // HD
    key_rows = gathered.shape[0]
    return pl.pallas_call(
        attention_kernel,
        grid=(heads,),
        out_shape=jax.ShapeDtypeStruct((rows, width), jnp.bfloat16),
        in_specs=[
            pl.BlockSpec((rows, HD), lambda h: (0, h)),
            pl.BlockSpec((rows, HD), lambda h: (0, 0)),
            pl.BlockSpec((key_rows, HD), lambda h: (0, h)),
            pl.BlockSpec((key_rows, HD), lambda h: (0, 2 * heads)),
            pl.BlockSpec((key_rows, HD), lambda h: (0, heads + h)),
        ],
        out_specs=pl.BlockSpec((rows, HD), lambda h: (0, h)),
        compiler_params=pltpu.CompilerParams(vmem_limit_bytes=50 * 1024 * 1024),
    )(queries, query_bias, gathered, gathered, gathered)


def hot_and_bias(cluster_of, pair_mask):
    clusters = pair_mask.shape[0]
    columns = jnp.arange(HD, dtype=jnp.int32)
    hot = cluster_of[:, None] == columns[None, :]
    mask_rows = jnp.dot(
        hot[:, :clusters].astype(jnp.bfloat16),
        (pair_mask != 0).astype(jnp.bfloat16),
        preferred_element_type=jnp.float32,
    )
    bias = jnp.where(mask_rows > 0.5, 0.0, NEG).astype(jnp.bfloat16)
    bias = jnp.pad(bias, ((0, 0), (0, HD - clusters)))
    return hot.astype(jnp.bfloat16), bias


def body(queries, keys, values, cluster_of, pair_mask, out_weight):
    hot, bias = hot_and_bias(cluster_of, pair_mask)
    together = jnp.concatenate([keys, values, hot], axis=1)
    gathered = lax.all_gather(together, "seq", axis=0, tiled=True)
    attn_tok = attention(queries, bias, gathered)
    terms = jnp.dot(attn_tok, out_weight, preferred_element_type=jnp.float32)
    return lax.psum_scatter(terms.astype(jnp.bfloat16), "grp", scatter_dimension=1, tiled=True)


def solution(mesh):
    in_specs = (P("seq", "grp"), P("seq", "grp"), P("seq", "grp"), P("seq"), P(), P("grp", None))
    out_specs = P("seq", "grp")
    return jax.shard_map(body, mesh=mesh, in_specs=in_specs, out_specs=out_specs, check_vma=False)
```

```python
import jax
import jax.numpy as jnp
from jax import lax
from jax.experimental import pallas as pl
from jax.experimental.pallas import tpu as pltpu
from jax.sharding import PartitionSpec as P

HD = 128
NEG = -1e30
LOG2E = 1.4426950408889634
SCALE = HD**-0.5 * LOG2E


def attention_kernel(query, query_bias, key, key_hot, value, out):
    left = jnp.concatenate([query[...], query_bias[...]], axis=1)
    right = jnp.concatenate([key[...], key_hot[...]], axis=1)
    scores = lax.dot_general(
        left, right, (((1,), (1,)), ((), ())), preferred_element_type=jnp.float32
    )
    top = jnp.max(scores, axis=1, keepdims=True) * SCALE
    weights = jnp.exp2(scores * SCALE - top)
    total = jnp.sum(weights, axis=1, keepdims=True)
    mixed = jnp.dot(weights.astype(jnp.bfloat16), value[...], preferred_element_type=jnp.float32)
    out[...] = (mixed / total).astype(jnp.bfloat16)


def attention(queries, query_bias, gathered):
    rows, width = queries.shape
    heads = width // HD
    key_rows = gathered.shape[0]
    return pl.pallas_call(
        attention_kernel,
        grid=(heads,),
        out_shape=jax.ShapeDtypeStruct((rows, width), jnp.bfloat16),
        in_specs=[
            pl.BlockSpec((rows, HD), lambda h: (0, h)),
            pl.BlockSpec((rows, HD), lambda h: (0, 0)),
            pl.BlockSpec((key_rows, HD), lambda h: (0, h)),
            pl.BlockSpec((key_rows, HD), lambda h: (0, 2 * heads)),
            pl.BlockSpec((key_rows, HD), lambda h: (0, heads + h)),
        ],
        out_specs=pl.BlockSpec((rows, HD), lambda h: (0, h)),
        compiler_params=pltpu.CompilerParams(vmem_limit_bytes=50 * 1024 * 1024),
    )(queries, query_bias, gathered, gathered, gathered)


def hot_and_bias(cluster_of, pair_mask):
    clusters = pair_mask.shape[0]
    columns = jnp.arange(HD, dtype=jnp.int32)
    hot = cluster_of[:, None] == columns[None, :]
    mask_rows = jnp.dot(
        hot[:, :clusters].astype(jnp.bfloat16),
        (pair_mask != 0).astype(jnp.bfloat16),
        preferred_element_type=jnp.float32,
    )
    bias = jnp.where(mask_rows > 0.5, 0.0, NEG).astype(jnp.bfloat16)
    bias = jnp.pad(bias, ((0, 0), (0, HD - clusters)))
    return hot.astype(jnp.bfloat16), bias


def gather_rows(shard):
    count = lax.axis_size("seq")
    outer = 1
    while outer * outer < count:
        outer *= 2
    inner = count // outer
    half = shard.shape[0] // 2

    def move(piece, outer_step, inner_step):
        pairs = []
        for o in range(outer):
            for i in range(inner):
                target = (o + outer_step) % outer * inner + (i + inner_step) % inner
                pairs.append((o * inner + i, target))
        return lax.ppermute(piece, "seq", pairs)

    pieces = [shard]
    upward, downward = shard[:half], shard[half:]
    for _ in range(outer - 1):
        upward, downward = move(upward, 1, 0), move(downward, -1, 0)
        pieces += [upward, downward]
    received = list(pieces)
    for piece in pieces:
        for _ in range(inner - 1):
            piece = move(piece, 0, 1)
            received.append(piece)
    return jnp.concatenate(received, axis=0)


def body(queries, keys, values, cluster_of, pair_mask, out_weight):
    hot, bias = hot_and_bias(cluster_of, pair_mask)
    together = jnp.concatenate([keys, values, hot], axis=1)
    gathered = gather_rows(together)
    attn_tok = attention(queries, bias, gathered)
    terms = jnp.dot(attn_tok, out_weight, preferred_element_type=jnp.float32)
    return lax.psum_scatter(terms.astype(jnp.bfloat16), "grp", scatter_dimension=1, tiled=True)


def solution(mesh):
    in_specs = (P("seq", "grp"), P("seq", "grp"), P("seq", "grp"), P("seq"), P(), P("grp", None))
    out_specs = P("seq", "grp")
    return jax.shard_map(body, mesh=mesh, in_specs=in_specs, out_specs=out_specs, check_vma=False)
```

```python
import jax
import jax.numpy as jnp
from jax import lax
from jax.experimental import pallas as pl
from jax.experimental.pallas import tpu as pltpu
from jax.sharding import PartitionSpec as P

HD = 128
NEG = -1e30
LOG2E = 1.4426950408889634
SCALE = HD**-0.5 * LOG2E


def attention_kernel(query, query_bias, key, key_hot, value, out):
    left = jnp.concatenate([query[...], query_bias[...]], axis=1)
    right = jnp.concatenate([key[...], key_hot[...]], axis=1)
    scores = lax.dot_general(
        left, right, (((1,), (1,)), ((), ())), preferred_element_type=jnp.float32
    )
    top = jnp.max(scores, axis=1, keepdims=True) * SCALE
    weights = jnp.exp2(scores * SCALE - top)
    total = jnp.sum(weights, axis=1, keepdims=True)
    mixed = jnp.dot(weights.astype(jnp.bfloat16), value[...], preferred_element_type=jnp.float32)
    out[...] = (mixed / total).astype(jnp.bfloat16)


def attention(queries, query_bias, gathered):
    rows, width = queries.shape
    heads = width // HD
    key_rows = gathered.shape[0]
    return pl.pallas_call(
        attention_kernel,
        grid=(heads,),
        out_shape=jax.ShapeDtypeStruct((rows, width), jnp.bfloat16),
        in_specs=[
            pl.BlockSpec((rows, HD), lambda h: (0, h)),
            pl.BlockSpec((rows, HD), lambda h: (0, 0)),
            pl.BlockSpec((key_rows, HD), lambda h: (0, h)),
            pl.BlockSpec((key_rows, HD), lambda h: (0, 2 * heads)),
            pl.BlockSpec((key_rows, HD), lambda h: (0, heads + h)),
        ],
        out_specs=pl.BlockSpec((rows, HD), lambda h: (0, h)),
        compiler_params=pltpu.CompilerParams(vmem_limit_bytes=50 * 1024 * 1024),
    )(queries, query_bias, gathered, gathered, gathered)


def hot_and_bias(cluster_of, pair_mask):
    clusters = pair_mask.shape[0]
    columns = jnp.arange(HD, dtype=jnp.int32)
    hot = cluster_of[:, None] == columns[None, :]
    mask_rows = jnp.dot(
        hot[:, :clusters].astype(jnp.bfloat16),
        (pair_mask != 0).astype(jnp.bfloat16),
        preferred_element_type=jnp.float32,
    )
    bias = jnp.where(mask_rows > 0.5, 0.0, NEG).astype(jnp.bfloat16)
    bias = jnp.pad(bias, ((0, 0), (0, HD - clusters)))
    return hot.astype(jnp.bfloat16), bias


def gather_rows(shard):
    count = lax.axis_size("seq")
    outer = 1
    while outer * outer < count:
        outer *= 2
    inner = count // outer
    half = shard.shape[0] // 2

    def move(piece, outer_step, inner_step):
        pairs = []
        for o in range(outer):
            for i in range(inner):
                target = (o + outer_step) % outer * inner + (i + inner_step) % inner
                pairs.append((o * inner + i, target))
        return lax.ppermute(piece, "seq", pairs)

    pieces = [shard]
    upward, downward = shard[:half], shard[half:]
    for _ in range(outer - 1):
        upward, downward = move(upward, 1, 0), move(downward, -1, 0)
        pieces += [upward, downward]
    received = list(pieces)
    crossed = shard
    for _ in range(inner - 1):
        crossed = move(crossed, 0, 1)
        received += [crossed, move(crossed[half:], 1, 0)]
    for piece in pieces[1:-1]:
        for _ in range(inner - 1):
            piece = move(piece, 0, 1)
            received.append(piece)
    return jnp.concatenate(received, axis=0)


def body(queries, keys, values, cluster_of, pair_mask, out_weight):
    hot, bias = hot_and_bias(cluster_of, pair_mask)
    together = jnp.concatenate([keys, values, hot], axis=1)
    gathered = gather_rows(together)
    attn_tok = attention(queries, bias, gathered)
    terms = jnp.dot(attn_tok, out_weight, preferred_element_type=jnp.float32)
    return lax.psum_scatter(terms.astype(jnp.bfloat16), "grp", scatter_dimension=1, tiled=True)


def solution(mesh):
    in_specs = (P("seq", "grp"), P("seq", "grp"), P("seq", "grp"), P("seq"), P(), P("grp", None))
    out_specs = P("seq", "grp")
    return jax.shard_map(body, mesh=mesh, in_specs=in_specs, out_specs=out_specs, check_vma=False)
```
